128 devices in a mesh: blk: 16 (over x, y_hi, core), enc: 8 (over y_lo, z).
Axes of the slice: x: 4, y: 4 (y_hi: 2, y_lo: 2; y = y_hi * 2 + y_lo), z: 4, core: 2. Of those that a mesh axis runs over, the one named last changes fastest.
Arguments:
- spectra: bfloat16 [16384, 28672], P('blk', 'enc'), may hold values from 0.0009994507 to 1
- wide_kernel: bfloat16 [96, 128], replicated, may hold values from -0.625 to 0.625
- deep_kernel: bfloat16 [1024, 256], replicated, may hold values from -0.1875 to 0.1875
- dense_weight: bfloat16 [28672, 256], P('enc'), may hold values from -0.03125 to 0.03125
- ref_embed: bfloat16 [65536, 256], P('blk'), may hold values from -6 to 6
- ref_coords: bfloat16 [65536, 64], P('blk'), may hold values from -18 to 18
- query_bucket: int32 [16384], P(('blk', 'enc')), may hold values from 0 to 31
- ref_bucket: int32 [65536], P('blk'), may hold values from 0 to 31, as said below
Outputs:
- projection: float32 [16384, 64], P(('blk', 'enc'))
The draws below stay inside these ranges and needn't reach their ends.
Inputs may be any that keep to these rules, and one draw needn't show every extreme that they name: `ref_bucket`: every bucket 0 to 31 is held by some reference.
All inputs are finite; a program needn't handle non-finite values.
Results may differ from the reference program's by a relative error of at most 0.038.
Values may be sent and summed in bfloat16 or wider, within the bound.
No kernel may reach another device: no remote copies, remote signals or barrier semaphores. Data moves between devices by JAX's collectives and lax.ppermute only.
A program may use at most 128 MiB of HBM per device.

```python
import math
import jax
import jax.numpy as jnp
from jax import lax

BINS = 28672
CH1 = 128
CH2 = 256
EMB = 256
COORD = 64
BUCKETS = 32
QUERIES = 16384
REFS = 65536


def draw_ref_bucket(key, part):
    base = jax.random.randint(jax.random.fold_in(key, 11), (REFS,), 0, BUCKETS).astype(jnp.int32)
    order = jax.random.permutation(jax.random.fold_in(key, 12), BUCKETS).astype(jnp.int32)
    return jnp.concatenate([order, base[BUCKETS:]])


def place_ends(values, rng, least, top_value):
    index_at = [jax.random.randint(jax.random.fold_in(rng, axis), (), 0, length) for axis, length in enumerate(values.shape)]
    widest = values.shape.index(max(values.shape))
    neighbour = index_at[:widest] + [(index_at[widest] + 1) % values.shape[widest]] + index_at[widest + 1:]
    return values.at[tuple(index_at)].set(least).at[tuple(neighbour)].set(top_value)


def level_of(own_key, extent, shards, low, largest):
    factor_of, own = 1.0, jax.random.fold_in(own_key, 6)
    for dim, shards_of in shards:
        heights = jnp.exp(jax.random.uniform(jax.random.fold_in(own, dim), (shards_of,), jnp.float32, low / len(shards), largest / len(shards)))
        factor_of = factor_of * jnp.repeat(heights, extent[dim] // shards_of).reshape([-1 if axis == dim else 1 for axis in range(len(extent))])
    return factor_of


def normal_values(rng, shape, spread, bound, shards=(), dtype=jnp.bfloat16):
    array = spread * jax.random.normal(rng, shape, jnp.float32)
    if shards:
        array = array * level_of(rng, shape, shards, -0.22, 0.18)
    return jnp.clip(array, -bound, bound).astype(dtype)


def setup_inputs(seed: int = 0) -> dict:
    splits = jax.random.split(jax.random.key(seed), 9)
    return {
        "spectra": jnp.clip(jnp.exp(math.log(1.0) - 6.9083047 * jax.random.uniform(splits[0], (QUERIES, BINS), jnp.float32) ** level_of(splits[0], (QUERIES, BINS), ((0, 16), (1, 8)), -0.2, 0.2)), 0.0009994507, 1.0).astype(jnp.bfloat16),
        "wide_kernel": normal_values(splits[1], (96, CH1), 96 ** -0.5, 0.625),
        "deep_kernel": normal_values(splits[2], (8 * CH1, CH2), (8 * CH1) ** -0.5, 0.1875),
        "dense_weight": normal_values(splits[3], (BINS // 256 * CH2, EMB), (BINS // 256 * CH2) ** -0.5, 0.03125, ((0, 8),)),
        "ref_embed": normal_values(splits[4], (REFS, EMB), 1.0, 6.0, ((0, 16),)),
        "ref_coords": normal_values(splits[5], (REFS, COORD), 3.0, 18.0, ((0, 16),)),
        "query_bucket": place_ends(jax.random.randint(splits[6], (QUERIES,), 0, BUCKETS), jax.random.fold_in(splits[6], 1), 0, BUCKETS - 1).astype(jnp.int32),
        "ref_bucket": draw_ref_bucket(jax.random.fold_in(splits[8], 71), 0),
    }


def encode_block(block, wide_kernel, deep_kernel):
    rows = block.shape[0]
    groups = block.reshape(rows, -1, 32)
    count = groups.shape[1] - 2
    windows = jnp.concatenate([groups[:, :count], groups[:, 1:count + 1], groups[:, 2:count + 2]], axis=2)
    first = jax.nn.relu(jnp.einsum('qpk,kc->qpc', windows.astype(jnp.float32), wide_kernel.astype(jnp.float32))).astype(jnp.bfloat16)
    stacked = first.reshape(rows, count // 8, -1)
    second = jax.nn.relu(jnp.einsum('qpk,kc->qpc', stacked.astype(jnp.float32), deep_kernel.astype(jnp.float32))).astype(jnp.bfloat16)
    return second.reshape(rows, -1)

def reference(spectra, wide_kernel, deep_kernel, dense_weight, ref_embed, ref_coords, query_bucket, ref_bucket):
    total_rows = spectra.shape[0]
    block_rows = 256 if total_rows % 256 == 0 else total_rows
    padded = jnp.pad(spectra, ((0, 0), (32, 32)))
    blocks = padded.reshape(total_rows // block_rows, block_rows, -1)
    features = lax.map(lambda b: encode_block(b, wide_kernel, deep_kernel), blocks)
    features = features.reshape(total_rows, -1)
    emb = jnp.dot(features, dense_weight, preferred_element_type=jnp.float32)
    unit_query = (emb * lax.rsqrt(lax.optimization_barrier(jnp.sum(emb * emb, axis=1, keepdims=True)) + 1e-06)).astype(jnp.bfloat16)
    refs = ref_embed.astype(jnp.float32)
    unit_ref = (refs * lax.rsqrt(lax.optimization_barrier(jnp.sum(refs * refs, axis=1, keepdims=True)) + 1e-06)).astype(jnp.bfloat16)
    ref_tags = ref_bucket.astype(jnp.float32)
    query_tags = query_bucket.astype(jnp.float32)

    def project(pair):
        rows, tags = pair
        scores = jnp.dot(rows, unit_ref.T, preferred_element_type=jnp.float32)
        allowed = jnp.abs(tags[:, None] - ref_tags[None, :]) <= 1.5
        weight = jnp.where(allowed, jnp.exp(40.0 * scores - 40.0), jnp.float32(0.0))
        total = lax.optimization_barrier(jnp.sum(weight, axis=1))
        moved = jnp.dot(weight.astype(jnp.bfloat16), ref_coords, preferred_element_type=jnp.float32)
        return moved / total[:, None]
    shaped = unit_query.reshape(total_rows // block_rows, block_rows, -1)
    shaped_tags = query_tags.reshape(total_rows // block_rows, block_rows)
    result = lax.map(project, (shaped, shaped_tags))
    return result.reshape(total_rows, -1)
```

```python
import functools

import jax
import jax.numpy as jnp
from jax import lax
from jax.experimental import pallas as pl
from jax.experimental.pallas import tpu as pltpu
from jax.sharding import PartitionSpec as P

F32, BF16 = jnp.float32, jnp.bfloat16
SCALE = 40.0 * 1.4426950408889634
LANES = 128
TAG_ROWS = 16


def relu(v):
    return jnp.maximum(v.astype(BF16), jnp.zeros((), BF16))


def params(mib=24):
    return pltpu.CompilerParams(vmem_limit_bytes=mib << 20)


def whole(shape):
    return pl.BlockSpec(shape, lambda *_: (0,) * len(shape), pipeline_mode=pl.Buffered(1))


def spread_taps(wide):
    taps, ch = wide.shape
    zeros = lambda n: jnp.zeros((n, ch), BF16)
    at = lambda off, size: jnp.concatenate([zeros(off), wide, zeros(size - off - taps)], 0)
    one = jnp.concatenate([at(0, 128), at(32, 128)], 1)
    two = jnp.concatenate([at(64, 256), at(96, 256)], 1)
    return one, two


def encode_body(me_ref, xa, xb, la, lb, ra, rb, one_ref, two_ref, deep_ref, dense_ref, out_ref, first, second):
    one, two = one_ref[...], two_ref[...]
    chunks = xa.shape[1] // LANES
    blocks = chunks // 2

    def chunk(c, n):
        parts = []
        for x, left, right in ((xa, la, ra), (xb, lb, rb)):
            if c < 0:
                parts.append(jnp.concatenate([left[...], x[:, :LANES]], 1))
            elif c + n > chunks:
                parts.append(jnp.concatenate([x[:, c * LANES :], right[...]], 1))
            else:
                parts.append(x[:, c * LANES : (c + n) * LANES])
        return jnp.concatenate(parts, 0)

    def pair_two(c):
        return relu(jnp.dot(chunk(c, 2), two, preferred_element_type=F32))

    def pair_one(c):
        return relu(jnp.dot(chunk(c, 1), one, preferred_element_type=F32))

    before = pair_two(-1)[:, LANES:]
    for i in range(blocks):
        after = pair_two(2 * i + 1)
        buf = first.at[i % 2]
        buf[:, 0:128] = before
        buf[:, 128:384] = pair_one(2 * i)
        buf[:, 384:640] = pair_two(2 * i)
        buf[:, 640:896] = pair_one(2 * i + 1)
        buf[:, 896:1024] = after[:, :LANES]
        before = after[:, LANES:]
        second[:, 256 * i : 256 * i + 256] = relu(
            jnp.dot(buf[...], deep_ref[...], preferred_element_type=F32)
        )
    out_ref[...] = jnp.dot(second[...], dense_ref[...], preferred_element_type=F32).astype(BF16)


def encode(me, step, spectra, left, right, one, two, deep, dense):
    rows, bins = 128, spectra.shape[1]
    near = lambda i, me: (me[0] ^ step, 0)
    far = lambda i, me: (me[0] ^ step ^ 4, 0)
    flops = 2 * 256 * (bins * 128 * 6 + bins * 1024 + bins * 256)
    return pl.pallas_call(
        encode_body,
        grid_spec=pltpu.PrefetchScalarGridSpec(
            num_scalar_prefetch=1,
            grid=(1,),
            in_specs=[
                pl.BlockSpec((rows, bins), near),
                pl.BlockSpec((rows, bins), far),
                pl.BlockSpec((rows, LANES), near),
                pl.BlockSpec((rows, LANES), far),
                pl.BlockSpec((rows, LANES), near),
                pl.BlockSpec((rows, LANES), far),
                whole(one.shape),
                whole(two.shape),
                whole(deep.shape),
                whole(dense.shape),
            ],
            out_specs=pl.BlockSpec((2 * rows, 256), lambda i, me: (0, 0)),
            scratch_shapes=[
                pltpu.VMEM((2, 2 * rows, 1024), BF16),
                pltpu.VMEM((2 * rows, bins), BF16),
            ],
        ),
        out_shape=jax.ShapeDtypeStruct((2 * rows, 256), BF16),
        compiler_params=params(),
        cost_estimate=pl.CostEstimate(flops=flops, bytes_accessed=5 << 20, transcendentals=0),
        name="encode",
    )(me, spectra, spectra, left, left, right, right, one, two, deep, dense)


def ref_prep_body(ref_ref, tag_ref, coord_ref, rt_ref, co_ref):
    r = ref_ref[...].astype(F32)
    unit = r * lax.rsqrt(jnp.sum(r * r, axis=1, keepdims=True) + 1e-06)
    rt_ref[0:256, :] = unit.astype(BF16).T
    rt_ref[256:, :] = jnp.broadcast_to(tag_ref[...].astype(F32), (TAG_ROWS, r.shape[0])).astype(BF16)
    n = coord_ref.shape[0]
    lane = lax.broadcasted_iota(jnp.int32, (n, 64), 1)
    ones = jnp.where(lane < 2, 1.0, 0.0).astype(BF16)
    co_ref[...] = jnp.concatenate([coord_ref[...], ones], 1)


def ref_prep(ref_embed, ref_bucket, ref_coords):
    n, emb = ref_embed.shape
    rows = 512
    return pl.pallas_call(
        ref_prep_body,
        grid=(n // rows,),
        in_specs=[
            pl.BlockSpec((rows, emb), lambda i: (i, 0)),
            pl.BlockSpec((1, rows), lambda i: (0, i)),
            pl.BlockSpec((rows, 64), lambda i: (i, 0)),
        ],
        out_specs=[
            pl.BlockSpec((emb + TAG_ROWS, rows), lambda i: (0, i)),
            pl.BlockSpec((rows, LANES), lambda i: (i, 0)),
        ],
        out_shape=[
            jax.ShapeDtypeStruct((emb + TAG_ROWS, n), BF16),
            jax.ShapeDtypeStruct((n, LANES), BF16),
        ],
        compiler_params=params(),
        cost_estimate=pl.CostEstimate(flops=1 << 20, bytes_accessed=8 << 20, transcendentals=0),
        name="ref_prep",
    )(ref_embed, ref_bucket.reshape(1, n), ref_coords)


def sum_enc_body(own, g1, g2, g3, tag_ref, keep_ref, send_ref):
    s = own[...].astype(F32) + g1[...].astype(F32) + g2[...].astype(F32) + g3[...].astype(F32)
    keep_ref[0:128, :] = s[:128].astype(BF16)
    tags = jnp.broadcast_to(tag_ref[...].astype(F32), (TAG_ROWS, 128)).astype(BF16)
    keep_ref[128:, :] = jnp.concatenate([tags, tags], 1)
    send_ref[...] = s[128:].astype(BF16)


def sum_enc(own, g1, g2, g3, query_bucket):
    return pl.pallas_call(
        sum_enc_body,
        out_shape=[
            jax.ShapeDtypeStruct((128 + TAG_ROWS, 256), BF16),
            jax.ShapeDtypeStruct((128, 256), BF16),
        ],
        compiler_params=params(),
        cost_estimate=pl.CostEstimate(flops=1 << 18, bytes_accessed=1 << 20, transcendentals=0),
        name="sum_enc",
    )(own, g1, g2, g3, query_bucket.reshape(1, 128))


def unit_body(keep, a, b, c, out_ref):
    for k, (u, v) in enumerate(((keep, a), (b, c))):
        e = u[0:128, :].astype(F32) + v[0:128, :].astype(F32)
        out_ref[144 * k : 144 * k + 128, :] = (
            e * lax.rsqrt(jnp.sum(e * e, axis=1, keepdims=True) + 1e-06)
        ).astype(BF16)
        out_ref[144 * k + 128 : 144 * k + 144, :] = u[128:144, :]


def unit_queries(keep, a, b, c):
    return pl.pallas_call(
        unit_body,
        out_shape=jax.ShapeDtypeStruct((2 * (128 + TAG_ROWS), 256), BF16),
        compiler_params=params(),
        cost_estimate=pl.CostEstimate(flops=1 << 18, bytes_accessed=1 << 20, transcendentals=0),
        name="unit_queries",
    )(keep, a, b, c)


def weigh_body(q_ref, rta, rtb, coa, cob, out_ref, acc, q_sc, tag_sc, *, width):
    j = pl.program_id(0)

    @pl.when(j == 0)
    def _():
        for k in range(2):
            q_sc[128 * k : 128 * k + 128, :] = q_ref[144 * k : 144 * k + 128, :]
            row = q_ref[144 * k + 128 : 144 * k + 144, 0:128].astype(F32)[0:1, :]
            tag_sc[128 * k : 128 * k + 128, :] = jnp.broadcast_to(row, (128, 128)).T.astype(BF16)

    q, tag = q_sc[...], tag_sc[...]
    tags = jnp.concatenate([tag] * (width // LANES), 1)
    total = None
    for rt, co in ((rta, coa), (rtb, cob)):
        for k in range(co.shape[0] // width):
            cols = slice(k * width, (k + 1) * width)
            s = jnp.dot(q, rt[0:256, cols], preferred_element_type=F32)
            w = jnp.exp2(s * SCALE - SCALE).astype(BF16)
            ok = jnp.abs(tags - rt[256:257, cols]) <= jnp.bfloat16(1.5)
            w = jnp.where(ok, w, jnp.zeros((), BF16))
            d = jnp.dot(w, co[cols, :], preferred_element_type=F32)
            total = d if total is None else total + d

    @pl.when(j == 0)
    def _():
        acc[...] = total

    @pl.when(j > 0)
    def _():
        acc[...] += total

    @pl.when(j == pl.num_programs(0) - 1)
    def _():
        a = acc[...]
        lane = lax.broadcasted_iota(jnp.int32, a.shape, 1)
        low = a - a.astype(BF16).astype(F32)
        out_ref[...] = jnp.where(lane == 65, low, a).astype(BF16)


def weigh(q, rta, rtb, coa, cob):
    n = coa.shape[0]
    block = 1024
    rt_spec = pl.BlockSpec((256 + TAG_ROWS, block), lambda j: (0, j))
    co_spec = pl.BlockSpec((block, LANES), lambda j: (j, 0))
    return pl.pallas_call(
        functools.partial(weigh_body, width=256),
        grid=(n // block,),
        in_specs=[whole(q.shape), rt_spec, rt_spec, co_spec, co_spec],
        out_specs=pl.BlockSpec((256, LANES), lambda j: (0, 0)),
        out_shape=jax.ShapeDtypeStruct((256, LANES), BF16),
        scratch_shapes=[
            pltpu.VMEM((256, LANES), F32),
            pltpu.VMEM((256, 256), BF16),
            pltpu.VMEM((256, LANES), BF16),
        ],
        compiler_params=params(),
        cost_estimate=pl.CostEstimate(
            flops=2 * 256 * 2 * n * 384, bytes_accessed=6 << 20, transcendentals=256 * 2 * n
        ),
        name="weigh",
    )(q, rta, rtb, coa, cob)


def add_body(own, g1, g2, g3, keep_ref, send_ref):
    s = own[...].astype(F32) + g1[...].astype(F32) + g2[...].astype(F32) + g3[...].astype(F32)
    keep_ref[...] = s[:128]
    s = s[128:]
    lane = lax.broadcasted_iota(jnp.int32, s.shape, 1)
    whole_total = s[:, 64:65] + s[:, 65:66]
    s = jnp.where((lane == 64) | (lane == 65), whole_total, s)
    low = s - s.astype(BF16).astype(F32)
    send_ref[...] = jnp.where(lane == 65, low, s).astype(BF16)


def add_parts(own, g1, g2, g3):
    return pl.pallas_call(
        add_body,
        out_shape=[
            jax.ShapeDtypeStruct((128, LANES), F32),
            jax.ShapeDtypeStruct((128, LANES), BF16),
        ],
        compiler_params=params(),
        cost_estimate=pl.CostEstimate(flops=1 << 18, bytes_accessed=1 << 19, transcendentals=0),
        name="add_parts",
    )(own, g1, g2, g3)


def finish_body(keep, got, out_ref):
    s = keep[...] + got[...].astype(F32)
    total = s[:, 64:65] + s[:, 65:66]
    out_ref[...] = s[:, 0:64] / total


def finish(keep, got):
    return pl.pallas_call(
        finish_body,
        out_shape=jax.ShapeDtypeStruct((128, 64), F32),
        compiler_params=params(),
        name="finish",
    )(keep, got)


def swap(value, blk_bits, enc_bits):
    blks, encs = lax.axis_size("blk"), lax.axis_size("enc")
    pairs = [
        (b * encs + e, (b ^ blk_bits) * encs + (e ^ enc_bits))
        for b in range(blks)
        for e in range(encs)
    ]
    return lax.ppermute(value, ("blk", "enc"), pairs)


def per_device(
    spectra, wide_kernel, deep_kernel, dense_weight, ref_embed, ref_coords, query_bucket, ref_bucket
):
    me = lax.axis_index("enc").astype(jnp.int32).reshape(1)
    encs = lax.axis_size("enc")
    up = [(i, i + 1) for i in range(encs - 1)]
    left = lax.ppermute(spectra[:, -LANES:], "enc", up)
    right = lax.ppermute(spectra[:, :LANES], "enc", [(j, i) for i, j in up])
    rt, co = ref_prep(ref_embed, ref_bucket, ref_coords)
    rt_peer, co_peer = swap(rt, 1, 0), swap(co, 1, 0)
    one, two = spread_taps(wide_kernel)
    parts, got = None, []
    for step in (2, 1, 3, 0):
        part = encode(me, step, spectra, left, right, one, two, deep_kernel, dense_weight)
        if step:
            got.append(swap(part, 0, step))
        else:
            own = part
    keep, send = sum_enc(own, *got, query_bucket)
    b = swap(keep, 2, 0)
    c = swap(send, 2, 4)
    a = swap(send, 0, 4)
    q = unit_queries(keep, a, b, c)
    visiting = [swap(q, 4 * k, 0) for k in (1, 3, 2)]
    own = weigh(q, rt, rt_peer, co, co_peer)
    back = [
        swap(weigh(v, rt, rt_peer, co, co_peer), 4 * k, 0) for k, v in zip((1, 3, 2), visiting)
    ]
    keep, send = add_parts(own, *back)
    return finish(keep, swap(send, 2, 0))


def solution(mesh):
    placed = (
        P("blk", "enc"),
        P(),
        P(),
        P("enc", None),
        P("blk", None),
        P("blk", None),
        P(("blk", "enc")),
        P("blk"),
    )
    return jax.shard_map(
        per_device, mesh=mesh, in_specs=placed, out_specs=P(("blk", "enc"), None), check_vma=False
    )
```

```python
import functools

import jax
import jax.numpy as jnp
from jax import lax
from jax.experimental import pallas as pl
from jax.experimental.pallas import tpu as pltpu
from jax.sharding import PartitionSpec as P


F32, BF16 = jnp.float32, jnp.bfloat16
SCALE = 40.0 * 1.4426950408889634
LANES = 128
TAG_ROWS = 16


def relu(v):
    return jnp.maximum(v.astype(BF16), jnp.zeros((), BF16))


def params(mib=24):
    return pltpu.CompilerParams(vmem_limit_bytes=mib << 20)


def on_chip(value):
    return pltpu.with_memory_space_constraint(value, pltpu.VMEM)


def off_chip(value):
    return pltpu.with_memory_space_constraint(value, pltpu.HBM)


def whole(shape):
    return pl.BlockSpec(shape, lambda *_: (0,) * len(shape), pipeline_mode=pl.Buffered(1))


def edges_body(me_ref, head, tail, wide, to_left, to_right, one, two):
    to_left[...] = head[...].T[0:32, :]
    to_right[...] = tail[...].T[96:128, :]
    w = wide[...]
    one[...] = jnp.zeros(one.shape, BF16)
    two[...] = jnp.zeros(two.shape, BF16)
    for ref, column, row in ((one, 0, 0), (one, 1, 32), (two, 0, 64), (two, 1, 96)):
        ref[row : row + 96, 128 * column : 128 * column + 128] = w


def edges(me, spectra, wide):
    rows, bins = spectra.shape
    last = bins // LANES - 1
    return pl.pallas_call(
        edges_body,
        grid_spec=pltpu.PrefetchScalarGridSpec(
            num_scalar_prefetch=1,
            grid=(1,),
            in_specs=[
                pl.BlockSpec((rows, LANES), lambda i, me: (0, 0)),
                pl.BlockSpec((rows, LANES), lambda i, me: (0, last)),
                whole(wide.shape),
            ],
            out_specs=[whole((32, rows)), whole((32, rows)), whole((128, 256)), whole((256, 256))],
        ),
        out_shape=[
            jax.ShapeDtypeStruct((32, rows), BF16),
            jax.ShapeDtypeStruct((32, rows), BF16),
            jax.ShapeDtypeStruct((128, 256), BF16),
            jax.ShapeDtypeStruct((256, 256), BF16),
        ],
        compiler_params=params(),
        cost_estimate=pl.CostEstimate(flops=1 << 18, bytes_accessed=1 << 20, transcendentals=0),
        name="edges",
    )(me, *[off_chip(a) for a in (spectra, spectra, wide)])


def encode_body(me_ref, xa, xb, la, lb, ra, rb, one_ref, two_ref, deep_ref, dense_ref, out_ref, first, second):
    one, two = one_ref[...], two_ref[...]
    chunks = xa.shape[1] // LANES
    blocks = chunks // 2
    pad = jnp.zeros((96, 128), BF16)

    def chunk(c, n):
        parts = []
        for x, left, right in ((xa, la, ra), (xb, lb, rb)):
            if c < 0:
                parts.append(jnp.concatenate([jnp.concatenate([pad, left[...]], 0).T, x[:, :LANES]], 1))
            elif c + n > chunks:
                parts.append(jnp.concatenate([x[:, c * LANES :], jnp.concatenate([right[...], pad], 0).T], 1))
            else:
                parts.append(x[:, c * LANES : (c + n) * LANES])
        return jnp.concatenate(parts, 0)

    def pair_two(c):
        return relu(jnp.dot(chunk(c, 2), two, preferred_element_type=F32))

    def pair_one(c):
        return relu(jnp.dot(chunk(c, 1), one, preferred_element_type=F32))

    before = pair_two(-1)[:, LANES:]
    for i in range(blocks):
        after = pair_two(2 * i + 1)
        buf = first.at[i % 2]
        buf[:, 0:128] = before
        buf[:, 128:384] = pair_one(2 * i)
        buf[:, 384:640] = pair_two(2 * i)
        buf[:, 640:896] = pair_one(2 * i + 1)
        buf[:, 896:1024] = after[:, :LANES]
        before = after[:, LANES:]
        second[:, 256 * i : 256 * i + 256] = relu(
            jnp.dot(buf[...], deep_ref[...], preferred_element_type=F32)
        )
    out_ref[...] = jnp.dot(second[...], dense_ref[...], preferred_element_type=F32).astype(BF16)


def encode(me, step, spectra, left, right, one, two, deep, dense):
    rows, bins = 128, spectra.shape[1]
    near = lambda i, me: (me[0] ^ step, 0)
    far = lambda i, me: (me[0] ^ step ^ 4, 0)
    flops = 2 * 256 * (bins * 128 * 6 + bins * 1024 + bins * 256)
    return pl.pallas_call(
        encode_body,
        grid_spec=pltpu.PrefetchScalarGridSpec(
            num_scalar_prefetch=1,
            grid=(1,),
            in_specs=[
                pl.BlockSpec((rows, bins), near),
                pl.BlockSpec((rows, bins), far),
                pl.BlockSpec((32, rows), lambda i, me: near(i, me)[::-1]),
                pl.BlockSpec((32, rows), lambda i, me: far(i, me)[::-1]),
                pl.BlockSpec((32, rows), lambda i, me: near(i, me)[::-1]),
                pl.BlockSpec((32, rows), lambda i, me: far(i, me)[::-1]),
                whole(one.shape),
                whole(two.shape),
                whole(deep.shape),
                whole(dense.shape),
            ],
            out_specs=pl.BlockSpec((2 * rows, 256), lambda i, me: (0, 0)),
            scratch_shapes=[
                pltpu.VMEM((2, 2 * rows, 1024), BF16),
                pltpu.VMEM((2 * rows, bins), BF16),
            ],
        ),
        out_shape=jax.ShapeDtypeStruct((2 * rows, 256), BF16),
        compiler_params=params(),
        cost_estimate=pl.CostEstimate(flops=flops, bytes_accessed=5 << 20, transcendentals=0),
        name="encode",
    )(me, *[on_chip(a) for a in (spectra, spectra, left, left, right, right, one, two, deep, dense)])


def prepare_body(
    ref_ref, tag_ref, coord_ref, x_in, deep_in, dense_in, rt_ref, co_ref, x_out, deep_out, dense_out
):
    x_out[...] = x_in[...]
    deep_out[...] = deep_in[...]
    dense_out[...] = dense_in[...]
    r = ref_ref[...].astype(F32)
    unit = r * lax.rsqrt(jnp.sum(r * r, axis=1, keepdims=True) + 1e-06)
    rt_ref[0:256, :] = unit.astype(BF16).T
    rt_ref[256:, :] = jnp.broadcast_to(tag_ref[...].astype(F32), (TAG_ROWS, r.shape[0])).astype(BF16)
    row = lax.broadcasted_iota(jnp.int32, coord_ref.shape, 0)
    ones = jnp.where(row < 2, 1.0, 0.0).astype(BF16)
    co_ref[...] = jnp.concatenate([coord_ref[...], ones], 0).T


def prepare(ref_embed, ref_bucket, ref_coords, spectra, deep, dense):
    n, emb = ref_embed.shape
    steps = 2
    across = lambda a: pl.BlockSpec((a.shape[0], a.shape[1] // steps), lambda i: (0, i))
    down = lambda a: pl.BlockSpec((a.shape[0] // steps, a.shape[1]), lambda i: (i, 0))
    args = [ref_embed, ref_bucket.reshape(1, n), ref_coords.T, spectra, deep, dense]
    rt = jax.ShapeDtypeStruct((emb + TAG_ROWS, n), BF16)
    co = jax.ShapeDtypeStruct((n, LANES), BF16)
    same = [jax.ShapeDtypeStruct(a.shape, a.dtype) for a in args[3:]]
    return pl.pallas_call(
        prepare_body,
        grid=(steps,),
        in_specs=[down(args[0]), across(args[1]), across(args[2])] + [down(a) for a in args[3:]],
        out_specs=[across(rt), down(co)] + [down(a) for a in same],
        out_shape=[rt, co] + same,
        compiler_params=params(),
        cost_estimate=pl.CostEstimate(flops=1 << 20, bytes_accessed=16 << 20, transcendentals=0),
        name="prepare",
    )(*[off_chip(a) for a in args])


def sum_enc_body(own, g1, g2, g3, tag_ref, keep_ref, send_ref):
    s = own[...].astype(F32) + g1[...].astype(F32) + g2[...].astype(F32) + g3[...].astype(F32)
    keep_ref[0:128, :] = s[:128].astype(BF16)
    tags = jnp.broadcast_to(tag_ref[...].astype(F32), (TAG_ROWS, 128)).astype(BF16)
    keep_ref[128:, :] = jnp.concatenate([tags, tags], 1)
    send_ref[...] = s[128:].astype(BF16)


def sum_enc(own, g1, g2, g3, query_bucket):
    return pl.pallas_call(
        sum_enc_body,
        out_shape=[
            jax.ShapeDtypeStruct((128 + TAG_ROWS, 256), BF16),
            jax.ShapeDtypeStruct((128, 256), BF16),
        ],
        compiler_params=params(),
        cost_estimate=pl.CostEstimate(flops=1 << 18, bytes_accessed=1 << 20, transcendentals=0),
        name="sum_enc",
    )(own, g1, g2, g3, query_bucket.reshape(1, 128))


def unit_body(keep, a, b, c, out_ref):
    for k, (u, v) in enumerate(((keep, a), (b, c))):
        e = u[0:128, :].astype(F32) + v[0:128, :].astype(F32)
        out_ref[144 * k : 144 * k + 128, :] = (
            e * lax.rsqrt(jnp.sum(e * e, axis=1, keepdims=True) + 1e-06)
        ).astype(BF16)
        out_ref[144 * k + 128 : 144 * k + 144, :] = u[128:144, :]


def unit_queries(keep, a, b, c):
    return pl.pallas_call(
        unit_body,
        out_shape=jax.ShapeDtypeStruct((2 * (128 + TAG_ROWS), 256), BF16),
        compiler_params=params(),
        cost_estimate=pl.CostEstimate(flops=1 << 18, bytes_accessed=1 << 20, transcendentals=0),
        name="unit_queries",
    )(keep, a, b, c)


def weigh_body(q_ref, rta, rtb, coa, cob, out_ref, acc, q_sc, tag_sc, *, width):
    j = pl.program_id(0)

    @pl.when(j == 0)
    def _():
        for k in range(2):
            q_sc[128 * k : 128 * k + 128, :] = q_ref[144 * k : 144 * k + 128, :]
            row = q_ref[144 * k + 128 : 144 * k + 144, 0:128].astype(F32)[0:1, :]
            tag_sc[128 * k : 128 * k + 128, :] = jnp.broadcast_to(row, (128, 128)).T.astype(BF16)

    q, tag = q_sc[...], tag_sc[...]
    tags = jnp.concatenate([tag] * (width // LANES), 1)
    total = None
    for rt, co in ((rta, coa), (rtb, cob)):
        for k in range(co.shape[0] // width):
            cols = slice(k * width, (k + 1) * width)
            s = jnp.dot(q, rt[0:256, cols], preferred_element_type=F32)
            w = jnp.exp2(s * SCALE - SCALE).astype(BF16)
            ok = jnp.abs(tags - rt[256:257, cols]) <= jnp.bfloat16(1.5)
            w = jnp.where(ok, w, jnp.zeros((), BF16))
            d = jnp.dot(w, co[cols, :], preferred_element_type=F32)
            total = d if total is None else total + d

    @pl.when(j == 0)
    def _():
        acc[...] = total

    @pl.when(j > 0)
    def _():
        acc[...] += total

    @pl.when(j == pl.num_programs(0) - 1)
    def _():
        a = acc[...]
        lane = lax.broadcasted_iota(jnp.int32, a.shape, 1)
        low = a - a.astype(BF16).astype(F32)
        out_ref[...] = jnp.where(lane == 65, low, a).astype(BF16)


def weigh(q, rta, rtb, coa, cob):
    n = coa.shape[0]
    block = 4096
    rt_spec = pl.BlockSpec((256 + TAG_ROWS, block), lambda j: (0, j))
    co_spec = pl.BlockSpec((block, LANES), lambda j: (j, 0))
    return pl.pallas_call(
        functools.partial(weigh_body, width=256),
        grid=(n // block,),
        in_specs=[whole(q.shape), rt_spec, rt_spec, co_spec, co_spec],
        out_specs=pl.BlockSpec((256, LANES), lambda j: (0, 0)),
        out_shape=jax.ShapeDtypeStruct((256, LANES), BF16),
        scratch_shapes=[
            pltpu.VMEM((256, LANES), F32),
            pltpu.VMEM((256, 256), BF16),
            pltpu.VMEM((256, LANES), BF16),
        ],
        compiler_params=params(),
        cost_estimate=pl.CostEstimate(
            flops=2 * 256 * 2 * n * 384, bytes_accessed=6 << 20, transcendentals=256 * 2 * n
        ),
        name="weigh",
    )(q, rta, rtb, coa, cob)


def add_body(own, g1, g2, g3, keep_ref, send_ref):
    s = own[...].astype(F32) + g1[...].astype(F32) + g2[...].astype(F32) + g3[...].astype(F32)
    keep_ref[...] = s[:128]
    s = s[128:]
    lane = lax.broadcasted_iota(jnp.int32, s.shape, 1)
    whole_total = s[:, 64:65] + s[:, 65:66]
    s = jnp.where((lane == 64) | (lane == 65), whole_total, s)
    low = s - s.astype(BF16).astype(F32)
    send_ref[...] = jnp.where(lane == 65, low, s).astype(BF16)


def add_parts(own, g1, g2, g3):
    return pl.pallas_call(
        add_body,
        out_shape=[
            jax.ShapeDtypeStruct((128, LANES), F32),
            jax.ShapeDtypeStruct((128, LANES), BF16),
        ],
        compiler_params=params(),
        cost_estimate=pl.CostEstimate(flops=1 << 18, bytes_accessed=1 << 19, transcendentals=0),
        name="add_parts",
    )(own, g1, g2, g3)


def finish_body(keep, got, out_ref):
    s = (keep[...] + got[...].astype(F32)).T
    out_ref[...] = s[0:64, :] / (s[64:65, :] + s[65:66, :])


def finish(keep, got):
    return pl.pallas_call(
        finish_body,
        out_shape=jax.ShapeDtypeStruct((64, 128), F32),
        compiler_params=params(),
        name="finish",
    )(keep, got).T


def swap(value, blk_bits, enc_bits):
    blks, encs = lax.axis_size("blk"), lax.axis_size("enc")
    pairs = [
        (b * encs + e, (b ^ blk_bits) * encs + (e ^ enc_bits))
        for b in range(blks)
        for e in range(encs)
    ]
    return lax.ppermute(value, ("blk", "enc"), pairs)


def per_device(
    spectra, wide_kernel, deep_kernel, dense_weight, ref_embed, ref_coords, query_bucket, ref_bucket
):
    me = lax.axis_index("enc").astype(jnp.int32).reshape(1)
    encs = lax.axis_size("enc")
    up = [(i, i + 1) for i in range(encs - 1)]
    to_left, to_right, one, two = edges(me, spectra, wide_kernel)
    left = lax.ppermute(to_right, "enc", up)
    right = lax.ppermute(to_left, "enc", [(j, i) for i, j in up])
    rt, co, x, deep, dense = prepare(
        ref_embed, ref_bucket, ref_coords, spectra, deep_kernel, dense_weight
    )
    rt_peer, co_peer = swap(rt, 1, 0), swap(co, 1, 0)
    got = []
    for step in (2, 1, 3, 0):
        part = encode(me, step, x, left, right, one, two, deep, dense)
        if step:
            got.append(swap(part, 0, step))
    keep, send = sum_enc(part, *got, query_bucket)
    b = swap(keep, 2, 0)
    c = swap(send, 2, 4)
    a = swap(send, 0, 4)
    q = unit_queries(keep, a, b, c)
    visiting = []
    for k in (1, 3, 2):
        visiting.append(swap(q, 4 * k, 0))
    own = weigh(q, rt, rt_peer, co, co_peer)
    back = [swap(weigh(v, rt, rt_peer, co, co_peer), 4 * k, 0) for k, v in zip((1, 3, 2), visiting)]
    keep, send = add_parts(own, *back)
    return finish(keep, swap(send, 2, 0))


def solution(mesh):
    placed = (
        P("blk", "enc"),
        P(),
        P(),
        P("enc", None),
        P("blk", None),
        P("blk", None),
        P(("blk", "enc")),
        P("blk"),
    )
    return jax.shard_map(
        per_device, mesh=mesh, in_specs=placed, out_specs=P(("blk", "enc"), None), check_vma=False
    )
```
